128 devices in a mesh: dp: 4 (over x_lo, core), code: 32 (over z, y, x_hi).
Axes of the slice: x: 4 (x_hi: 2, x_lo: 2; x = x_hi * 2 + x_lo), y: 4, z: 4, core: 2. Of those that a mesh axis runs over, the one named last changes fastest.
Arguments:
- image_tokens: bfloat16 [16384, 1024], P(('dp', 'code')), may hold values from -6 to 6
- w_in: bfloat16 [1024, 4096], replicated, as said below
- w_out: bfloat16 [4096, 1024], replicated, as said below
- w_proj: bfloat16 [1024, 256], replicated, as said below
- codebook: bfloat16 [131072, 256], P('code'), may hold values from -6 to 6
- inv_temp: float32 [16384], replicated, may hold values from 4 to 240, as said below
- prior_mass: float32 [131072], P('code'), may hold values from 0.02 to 0.2
Outputs:
- refit_codes: float32 [131072, 256], P(('code', 'dp'))
- code_mass: float32 [131072], P(('code', 'dp'))
The draws below stay inside these ranges and needn't reach their ends.
Inputs may be any that keep to these rules, and one draw needn't show every extreme that they name: `inv_temp`: positive inverse temperatures. `w_in`: every entry lies within 6 / sqrt(1024) of zero. `w_out`: every entry lies within 6 / sqrt(4096) of zero. `w_proj`: every entry lies within 6 / sqrt(1024) of zero.
All inputs are finite; a program needn't handle non-finite values.
Results may differ from the reference program's by a relative error of at most 0.003.
The reference program's roundings to bfloat16 on the way (of `normed`, `hidden`, `encoded`, `unit_tokens`, `unit_codes` and `resp`) count: a program that leaves them out, or rounds other values in their place, can miss the bound.
Values may be sent and summed in bfloat16 or wider, within the bound.
A program may use at most 128 MiB of HBM per device.

```python
import math
import jax
import jax.numpy as jnp
from jax import lax

D = 1024
FF = 4096
E = 256
CODES = 131072
TOKENS = 16384


def tokens_law(key):
    sub = jax.random.fold_in(key, 1)
    values = jax.random.truncated_normal(sub, -6.0, 6.0, (TOKENS, D), jnp.float32)
    return values


def weight_law(key, label, rows, cols):
    sub = jax.random.fold_in(key, label)
    return jax.random.truncated_normal(sub, -6.0, 6.0, (rows, cols), jnp.float32) * (1.0 / math.sqrt(rows))


def draw_image_tokens(key, part):
    return tokens_law(key).astype(jnp.bfloat16)


def draw_w_in(key, part):
    return weight_law(key, 2, D, FF).astype(jnp.bfloat16)


def draw_w_out(key, part):
    return weight_law(key, 3, FF, D).astype(jnp.bfloat16)


def draw_w_proj(key, part):
    return weight_law(key, 4, D, E).astype(jnp.bfloat16)


def draw_codebook(key, part):
    values = jax.random.truncated_normal(jax.random.fold_in(key, 5), -6.0, 6.0, (CODES, E), jnp.float32)
    return values.astype(jnp.bfloat16)


def draw_inv_temp(key, part):
    values = jnp.exp(jax.random.uniform(jax.random.fold_in(key, 6), (TOKENS,), jnp.float32, jnp.log(4.0), jnp.log(40.0)))
    return values.astype(jnp.float32)


def block_scale(key, extent, cuts, low, largest):
    def one(position, shards_of):
        draws = jax.random.uniform(jax.random.fold_in(jax.random.fold_in(key, 6), position), (shards_of,), jnp.float32, low / len(cuts), largest / len(cuts))
        return jnp.repeat(jnp.exp(draws), extent[position] // shards_of).reshape((-1,) + (1,) * (len(extent) - position - 1))

    loudness = one(*cuts[0])
    for cut in cuts[1:]:
        loudness = loudness * one(*cut)
    return loudness


def setup_inputs(seed: int = 0) -> dict:
    seeds = jax.random.split(jax.random.key(seed), 8)
    image_tokens = draw_image_tokens(jax.random.fold_in(seeds[7], 71), 0)
    w_in = draw_w_in(jax.random.fold_in(seeds[7], 71), 0)
    w_out = draw_w_out(jax.random.fold_in(seeds[7], 71), 0)
    w_proj = draw_w_proj(jax.random.fold_in(seeds[7], 71), 0)
    codebook = draw_codebook(jax.random.fold_in(seeds[7], 71), 0)
    inv_temp = draw_inv_temp(jax.random.fold_in(seeds[7], 71), 0)
    prior_mass = jnp.clip(jnp.exp(math.log(0.2) - 2.3025851 * jax.random.uniform(seeds[6], (CODES,), jnp.float32) ** block_scale(seeds[6], (CODES,), ((0, 32),), -0.2, 0.2)), 0.02, 0.2)
    return {"image_tokens": image_tokens, "w_in": w_in, "w_out": w_out, "w_proj": w_proj, "codebook": codebook, "inv_temp": inv_temp, "prior_mass": prior_mass}


def unit_rows(matrix_f32):
    return matrix_f32 * lax.rsqrt(lax.optimization_barrier(jnp.mean(matrix_f32 * matrix_f32, axis=1, keepdims=True)) + 1e-06)

def encode(image_tokens, w_in, w_out, w_proj):
    tokens_f = image_tokens.astype(jnp.float32)
    mean = lax.optimization_barrier(jnp.mean(tokens_f, axis=1, keepdims=True))
    centered = tokens_f - mean
    var = lax.optimization_barrier(jnp.mean(centered * centered, axis=1, keepdims=True))
    normed = (centered * lax.rsqrt(var + 1e-06)).astype(jnp.bfloat16)
    hidden = jax.nn.gelu(jnp.dot(normed, w_in, preferred_element_type=jnp.float32), approximate=False).astype(jnp.bfloat16)
    encoded = (tokens_f + jnp.dot(hidden, w_out, preferred_element_type=jnp.float32)).astype(jnp.bfloat16)
    projected = jnp.dot(encoded, w_proj, preferred_element_type=jnp.float32)
    width = projected.shape[1]
    factor = jnp.sqrt(width / (lax.optimization_barrier(jnp.sum(projected * projected, axis=1, keepdims=True)) + 1e-06))
    return (projected * factor).astype(jnp.bfloat16)

def reference(image_tokens, w_in, w_out, w_proj, codebook, inv_temp, prior_mass):
    unit_tokens = encode(image_tokens, w_in, w_out, w_proj)
    unit_codes = unit_rows(codebook.astype(jnp.float32)).astype(jnp.bfloat16)
    total = unit_tokens.shape[0]
    width = unit_tokens.shape[1]
    block = math.gcd(total, 512)
    count = total // block
    scale = inv_temp * (1.0 / width)
    token_blocks = unit_tokens.reshape(count, block, width)
    scale_blocks = scale.reshape(count, block)

    def logits_of(token_block, scale_block):
        return jnp.dot(token_block, unit_codes.T, preferred_element_type=jnp.float32) * scale_block[:, None]

    def norm_of(pair):
        logits = logits_of(pair[0], pair[1])
        peak = lax.optimization_barrier(jnp.max(logits, axis=1))
        return peak + jnp.log(lax.optimization_barrier(jnp.sum(jnp.exp(logits - peak[:, None]), axis=1)))
    lognorm = lax.map(norm_of, (token_blocks, scale_blocks))

    def accumulate(carry, items):
        token_block, scale_block, norm_block = items
        resp = jnp.exp(logits_of(token_block, scale_block) - norm_block[:, None]).astype(jnp.bfloat16)
        sums = carry[0] + lax.dot_general(resp, token_block, (((0,), (0,)), ((), ())), preferred_element_type=jnp.float32)
        mass = carry[1] + lax.optimization_barrier(jnp.sum(resp.astype(jnp.float32), axis=0))
        return ((sums, mass), None)
    start = (jnp.zeros((codebook.shape[0], width), jnp.float32), jnp.zeros((codebook.shape[0],), jnp.float32))
    (sums, mass), _ = lax.scan(accumulate, start, (token_blocks, scale_blocks, lognorm))
    refit = (prior_mass[:, None] * codebook.astype(jnp.float32) + sums) / (prior_mass + mass)[:, None]
    return (refit, mass)
```

```python
import functools

import jax
import jax.numpy as jnp
from jax import lax
from jax.experimental import pallas as pl
from jax.experimental.pallas import tpu as pltpu
from jax.sharding import PartitionSpec as P

LOG2E = 1.4426950408889634
F32 = jnp.float32
BF16 = jnp.bfloat16
FT = 512
CH = 512
CB = 512
VMEM_LIMIT = 67043328


def encode_kernel(x_ref, win_ref, wout_ref, wproj_ref, o_ref, normed, acc):
    step = pl.program_id(0)

    @pl.when(step == 0)
    def _():
        x = x_ref[...].astype(F32)
        mean = jnp.mean(x, axis=1, keepdims=True)
        centered = x - mean
        var = jnp.mean(centered * centered, axis=1, keepdims=True)
        normed[...] = (centered * lax.rsqrt(var + 1e-06)).astype(BF16)
        acc[...] = jnp.zeros_like(acc)

    h = jnp.dot(normed[...], win_ref[...], preferred_element_type=F32)
    h = (0.5 * h * (1.0 + lax.erf(h * 0.7071067811865476))).astype(BF16)
    acc[...] += jnp.dot(h, wout_ref[...], preferred_element_type=F32)

    @pl.when(step == pl.num_programs(0) - 1)
    def _():
        encoded = (x_ref[...].astype(F32) + acc[...]).astype(BF16)
        projected = jnp.dot(encoded, wproj_ref[...], preferred_element_type=F32)
        width = projected.shape[1]
        factor = jnp.sqrt(width / (jnp.sum(projected * projected, axis=1, keepdims=True) + 1e-06))
        o_ref[...] = (projected * factor).astype(BF16)


def encode(x, w_in, w_out, w_proj):
    rows, d = x.shape
    ff, e = w_in.shape[1], w_proj.shape[1]
    return pl.pallas_call(
        encode_kernel,
        grid=(ff // FT,),
        in_specs=[
            pl.BlockSpec((rows, d), lambda i: (0, 0)),
            pl.BlockSpec((d, FT), lambda i: (0, i)),
            pl.BlockSpec((FT, d), lambda i: (i, 0)),
            pl.BlockSpec((d, e), lambda i: (0, 0)),
        ],
        out_specs=pl.BlockSpec((rows, e), lambda i: (0, 0)),
        out_shape=jax.ShapeDtypeStruct((rows, e), BF16),
        scratch_shapes=[pltpu.VMEM((rows, d), BF16), pltpu.VMEM((rows, d), F32)],
        name="encode",
    )(x, w_in, w_out, w_proj)


ORDER_A = [(0, 0), (1, 0), (3, 0), (0, 1), (1, 1), (3, 1), (2, 0), (2, 1)]
ORDER_B = [(0, 0), (0, 1), (1, 0), (1, 1), (3, 0), (3, 1), (2, 0), (2, 1)]


def pick(i, values):
    out = i * 0 + values[0]
    for k, v in enumerate(values[1:], 1):
        out = out + (i == k).astype(jnp.int32) * (v - values[0])
    return out


def refit_kernel(
    ut_ref, book_ref, inv_ref, prior_ref,
    out_ref, mass_ref,
    u_all, codes, p, ls0, ls1, lse, mloc, lx, ly, lz, u2,
    rc, rcm, rx, rxm, sx, sm, totals,
    ag_send, ag_recv, st_send, st_recv, rs_send, rs_recv,
):
    n_codes, width = book_ref.shape
    n_blocks = 16
    tb_size = 256
    dp = lax.axis_index("dp")
    code = lax.axis_index("code")
    h = lax.rem(code, 2)
    y = lax.rem(code // 2, 4)
    z = code // 8
    core = lax.rem(dp, 2)
    xlo = dp // 2

    zs = [lax.rem(z + d, 4) for d in range(4)]
    ys = [lax.rem(y + d, 4) for d in range(4)]

    def at(dz, dy, flip=0):
        hh = 1 - h if flip else h
        return (dp, (zs[dz] * 4 + ys[dy]) * 2 + hh)

    partner = (xlo * 2 + (1 - core), code)
    across = ((1 - xlo) * 2 + core, code)

    barrier = pltpu.get_barrier_semaphore()
    peers = [at(0, 0, 1), partner, across]
    peers += [at(d, 0) for d in (1, 2, 3)] + [at(0, d) for d in (1, 2, 3)]
    for peer in peers:
        pl.semaphore_signal(barrier, inc=1, device_id=peer, device_id_type=pl.DeviceIdType.MESH)
    pl.semaphore_wait(barrier, len(peers))

    sent = []

    def place(color, dz, dy):
        return color * 16 + zs[dz % 4] * 4 + ys[dy % 4]

    def view(index, half):
        if half is None:
            return u_all.at[index]
        return u_all.at[index, pl.ds(64 * half, 64)]

    def copy(src, dst, color, dz, dy, half, to):
        slot = ((color * 4 + dz % 4) * 4 + dy % 4) * 2 + (half or 0)
        c = pltpu.make_async_remote_copy(
            src_ref=src, dst_ref=dst, send_sem=ag_send.at[len(sent)], recv_sem=ag_recv.at[slot],
            device_id=to, device_id_type=pl.DeviceIdType.MESH,
        )
        sent.append(half)
        c.start()

    def send(color, dz, dy, half, ez, ey):
        ref = view(place(color, dz, dy), half)
        copy(ref, ref, color, dz - ez, dy - ey, half, at(ez % 4, ey % 4))

    def arrived(color, dz, dy, half=None):
        slot = ((color * 4 + dz) * 4 + dy) * 2 + (half or 0)
        ref = view(place(color, dz, dy), half)
        pltpu.make_async_remote_copy(
            src_ref=ref, dst_ref=ref, send_sem=ag_send.at[0], recv_sem=ag_recv.at[slot],
            device_id=at(1, 0), device_id_type=pl.DeviceIdType.MESH,
        ).wait_recv()

    def both(color, dz, dy, axis):
        for sign in (1, -1):
            send(color, dz, dy, None, *((sign, 0) if axis == "z" else (0, sign)))

    def onward(color, dz, dy, axis):
        arrived(color, dz, dy)
        step = dz if axis == "z" else dy
        half, sign = (0, -1) if step == 1 else (1, 1)
        send(color, dz, dy, half, *((sign, 0) if axis == "z" else (0, sign)))

    def halves(color, dz, dy):
        arrived(color, dz, dy, 0)
        arrived(color, dz, dy, 1)

    def c_start():
        ref = view(place(0, 0, 0), None)
        own = pltpu.make_async_copy(ut_ref, ref, rs_send.at[0])
        own.start()
        own.wait()
        copy(ref, view(place(1, 0, 0), None), 1, 0, 0, None, at(0, 0, 1))
        both(0, 0, 0, "y")
        both(0, 0, 0, "z")

    def c_first():
        for d in (1, 3):
            onward(0, 0, d, "y")
        for d in (1, 3):
            onward(0, d, 0, "z")
            both(0, d, 0, "y")

    def c0():
        arrived(1, 0, 0)
        both(1, 0, 0, "y")
        both(1, 0, 0, "z")
        for d in (1, 3):
            onward(0, 1, d, "y")

    def c1():
        for d in (1, 3):
            onward(0, 3, d, "y")
        halves(0, 2, 0)
        both(0, 2, 0, "y")

    def c2():
        halves(0, 0, 2)
        for d in (1, 3):
            onward(1, 0, d, "y")
            both(1, 0, d, "z")
        for d in (1, 3):
            onward(1, d, 0, "z")

    def c3():
        halves(0, 1, 2)

    def c4():
        halves(0, 3, 2)
        for d in (1, 3):
            onward(0, 2, d, "y")
        halves(1, 0, 2)
        both(1, 0, 2, "z")

    def c5():
        for e in (1, 3):
            for d in (1, 3):
                onward(1, e, d, "z")

    def c6():
        halves(0, 2, 2)

    def c7():
        for e in (1, 3):
            onward(1, e, 2, "z")

    def c13():
        halves(1, 2, 0)
        halves(1, 2, 1)
        halves(1, 2, 3)

    def c14():
        halves(1, 2, 2)

    comm = {0: c0, 1: c1, 2: c2, 3: c3, 4: c4, 5: c5, 6: c6, 7: c7, 13: c13, 14: c14}

    c_start()

    def unit_body(i, _):
        r = pl.ds(pl.multiple_of(i * 256, 256), 256)
        b = book_ref[r, :].astype(F32)
        codes[r, :] = (b * lax.rsqrt(jnp.mean(b * b, axis=1, keepdims=True) + 1e-06)).astype(BF16)
        return 0

    lax.fori_loop(0, n_codes // 256, unit_body, 0)
    c_first()

    rel_z = [a for a, _ in ORDER_A + ORDER_B]
    rel_p = [b for _, b in ORDER_A + ORDER_B]

    def block_at(i):
        color = i // 8
        zz = lax.rem(z + pick(i, rel_z), 4)
        pair = lax.rem(y // 2 + pick(i, rel_p), 2)
        hh = jnp.where(color == 0, h, 1 - h)
        return color * 8 + zz * 2 + pair, dp * 32 + (zz * 4 + pair * 2) * 2 + hh

    neg = jnp.full((8, tb_size), -jnp.inf, F32)

    def logits_of(tb, q, dest, peak):
        tokens = u_all[pl.ds(2 * tb, 2)].reshape(tb_size, width)
        l = lax.dot_general(
            codes[q * CH:(q + 1) * CH, :], tokens, (((1,), (1,)), ((), ())), preferred_element_type=F32
        )
        dest[q * CH:(q + 1) * CH, :] = l
        return jnp.maximum(peak, jnp.max(l.reshape(CH // 8, 8, tb_size), axis=0))

    def step(i, peak8, cur, nxt):
        tb, row = block_at(i)
        nxt_tb, _ = block_at(jnp.minimum(i + 1, n_blocks - 1))
        scale = jnp.concatenate([inv_ref[pl.ds(row, 1), :], inv_ref[pl.ds(row + 2, 1), :]], axis=1)
        scale = scale * (LOG2E / width)
        peak = jnp.max(peak8, axis=0, keepdims=True) * scale
        columns = pl.ds(pl.multiple_of(tb * tb_size, tb_size), tb_size)
        new_peak = neg
        total = jnp.zeros((8, tb_size), F32)
        for q in range(n_codes // CH):
            new_peak = logits_of(nxt_tb, q, nxt, new_peak)
            e = jnp.exp2(cur[q * CH:(q + 1) * CH, :] * scale - peak)
            p[q * CH:(q + 1) * CH, columns] = e.astype(BF16)
            total = total + jnp.sum(e.reshape(CH // 8, 8, tb_size), axis=0)
        mloc[tb] = peak
        lse[tb] = peak + jnp.log2(jnp.sum(total, axis=0, keepdims=True))
        return new_peak

    first, _ = block_at(h * 0)
    peak = neg
    for q in range(n_codes // CH):
        peak = logits_of(first, q, ls0, peak)

    def two_steps(j, peak8):
        for s, (cur, nxt) in enumerate(((ls0, ls1), (ls1, ls0))):
            for k, fn in comm.items():
                if k % 2 == s:
                    pl.when(j == k // 2)(fn)
            peak8 = step(2 * j + s, peak8, cur, nxt)
        return peak8

    lax.fori_loop(0, n_blocks // 2, two_steps, peak)

    stat_sent = []

    def stat_send(src, dst, slot, to):
        c = pltpu.make_async_remote_copy(
            src_ref=src, dst_ref=dst, send_sem=st_send.at[slot], recv_sem=st_recv.at[slot],
            device_id=to, device_id_type=pl.DeviceIdType.MESH,
        )
        stat_sent.append(c)
        c.start()
        return c

    cx = [
        stat_send(lse.at[pl.ds(0, 8)], lx.at[pl.ds(8, 8)], 0, at(0, 0, 1)),
        stat_send(lse.at[pl.ds(8, 8)], lx.at[pl.ds(0, 8)], 1, at(0, 0, 1)),
    ]
    for c in cx:
        c.wait()
    parts = [lse[...], lx[...]]
    top = jnp.maximum(*parts)
    ly[0] = top + jnp.log2(sum(jnp.exp2(v - top) for v in parts))
    cy = [stat_send(ly.at[0], ly.at[d], 1 + d, at(0, d)) for d in (1, 2, 3)]
    for c in cy:
        c.wait()
    parts = [ly[d] for d in range(4)]
    top = functools.reduce(jnp.maximum, parts)
    lz[0] = top + jnp.log2(sum(jnp.exp2(v - top) for v in parts))
    cz = [stat_send(lz.at[0], lz.at[d], 4 + d, at(d, 0)) for d in (1, 2, 3)]
    for c in cz:
        c.wait()
    parts = [lz[d] for d in range(4)]
    top = functools.reduce(jnp.maximum, parts)
    mloc[...] = jnp.exp2(mloc[...] - (top + jnp.log2(sum(jnp.exp2(v - top) for v in parts))))

    for k, half in enumerate(sent):
        ref = view(place(0, 0, 0), half)
        pltpu.make_async_remote_copy(
            src_ref=ref, dst_ref=ref, send_sem=ag_send.at[k], recv_sem=ag_recv.at[0],
            device_id=at(1, 0), device_id_type=pl.DeviceIdType.MESH,
        ).wait_send()

    def scale_body(tb, _):
        w = jnp.broadcast_to(mloc[tb], (128, tb_size)).T
        w = jnp.concatenate([w, w], axis=1)
        rows = pl.ds(pl.multiple_of(tb * tb_size, tb_size), tb_size)
        tokens = u_all[pl.ds(2 * tb, 2)].reshape(tb_size, width)
        u2[rows, :] = (tokens.astype(F32) * w).astype(BF16)
        return 0

    lax.fori_loop(0, n_blocks, scale_body, 0)

    ones = jnp.ones((8, 128), F32)
    per = n_codes // 4
    subs = per // CB

    def sums_of(first_row):
        r = pl.ds(pl.multiple_of(first_row, CB), CB)
        s = jnp.dot(p[r, :], u2[...], preferred_element_type=F32)
        acc = jnp.zeros((CB, 128), F32)
        for j in range(n_blocks * 2):
            acc = acc + p[r, j * 128:(j + 1) * 128].astype(F32) * mloc[j // 2][:, (j % 2) * 128:(j % 2) * 128 + 128]
        m = lax.dot_general(
            ones, acc, (((1,), (1,)), ((), ())), preferred_element_type=F32, precision=lax.Precision.HIGHEST
        )
        return s, m

    def reduce_send(src, dst, slot, to):
        c = pltpu.make_async_remote_copy(
            src_ref=src, dst_ref=dst, send_sem=rs_send.at[slot], recv_sem=rs_recv.at[slot],
            device_id=to, device_id_type=pl.DeviceIdType.MESH,
        )
        c.start()
        return c

    stage = ls0

    for side in range(2):
        chip = (1 - xlo) if side == 0 else xlo
        theirs = (chip * 2 + (1 - core)) * per
        ours = (chip * 2 + core) * per

        def side_body(b, _, side=side, theirs=theirs, ours=ours):
            slot = side * subs + b
            rows = pl.ds(pl.multiple_of(slot * CB, CB), CB)
            s, m = sums_of(theirs + b * CB)
            stage[rows, :] = s
            sm[slot] = m
            c1 = reduce_send(stage.at[rows], rc.at[slot], slot, partner)
            c2 = reduce_send(sm.at[slot], rcm.at[slot], 4 + slot, partner)
            s, m = sums_of(ours + b * CB)
            c1.wait_recv()
            c2.wait_recv()
            s = s + rc[slot]
            m = m + rcm[slot]
            if side == 0:
                sx[b] = s.astype(BF16)
                sm[4 + b] = m
                reduce_send(sx.at[b], rx.at[b], 8 + b, across)
                reduce_send(sm.at[4 + b], rxm.at[b], 10 + b, across)
            else:
                totals[b] = s
                sm[4 + subs + b] = m
            return 0

        lax.fori_loop(0, subs, side_body, 0)

    def column(row):
        c = jnp.broadcast_to(row, (128, 128)).T
        return jnp.concatenate([c, c], axis=1)

    for b in range(subs):
        pltpu.make_async_remote_copy(
            src_ref=sx.at[b], dst_ref=rx.at[b], send_sem=rs_send.at[8 + b], recv_sem=rs_recv.at[8 + b],
            device_id=across, device_id_type=pl.DeviceIdType.MESH).wait_recv()
        pltpu.make_async_remote_copy(
            src_ref=sm.at[4 + b], dst_ref=rxm.at[b], send_sem=rs_send.at[10 + b], recv_sem=rs_recv.at[10 + b],
            device_id=across, device_id_type=pl.DeviceIdType.MESH).wait_recv()
        m = sm[4 + subs + b] + rxm[b]
        for k in range(CB // 128):
            local = b * CB + k * 128
            part = slice(k * 128, (k + 1) * 128)
            index = b * (CB // 128) + k
            m_row = m[0:1, part]
            mass_ref[index:index + 1, :] = m_row
            prior = column(prior_ref[pl.ds(dp * (per // 128) + index, 1), :])
            book = book_ref[pl.ds(pl.multiple_of(dp * per + local, 128), 128), :].astype(F32)
            s = totals[b, part, :] + rx[b, part, :].astype(F32)
            out_ref[local:local + 128, :] = (prior * book + s) / (prior + column(m_row))

    for slot in range(2 * subs):
        pltpu.make_async_remote_copy(
            src_ref=stage.at[pl.ds(slot * CB, CB)], dst_ref=rc.at[slot], send_sem=rs_send.at[slot],
            recv_sem=rs_recv.at[slot], device_id=partner, device_id_type=pl.DeviceIdType.MESH).wait_send()
        pltpu.make_async_remote_copy(
            src_ref=sm.at[slot], dst_ref=rcm.at[slot], send_sem=rs_send.at[4 + slot],
            recv_sem=rs_recv.at[4 + slot], device_id=partner, device_id_type=pl.DeviceIdType.MESH).wait_send()
    for b in range(subs):
        pltpu.make_async_remote_copy(
            src_ref=sx.at[b], dst_ref=rx.at[b], send_sem=rs_send.at[8 + b], recv_sem=rs_recv.at[8 + b],
            device_id=across, device_id_type=pl.DeviceIdType.MESH).wait_send()
        pltpu.make_async_remote_copy(
            src_ref=sm.at[4 + b], dst_ref=rxm.at[b], send_sem=rs_send.at[10 + b], recv_sem=rs_recv.at[10 + b],
            device_id=across, device_id_type=pl.DeviceIdType.MESH).wait_send()


def refit(unit_tokens, codebook, inv_temp, prior_mass):
    n_codes, width = codebook.shape
    tokens = unit_tokens.shape[0] * 32
    per = n_codes // 4
    subs = per // CB
    vmem = pl.BlockSpec(memory_space=pltpu.VMEM)
    out, mass = pl.pallas_call(
        refit_kernel,
        in_specs=[vmem] * 4,
        out_specs=[vmem] * 2,
        out_shape=[
            jax.ShapeDtypeStruct((per, width), F32),
            jax.ShapeDtypeStruct((per // 128, 128), F32),
        ],
        scratch_shapes=[
            pltpu.VMEM((32, 128, width), BF16),
            pltpu.VMEM((n_codes, width), BF16),
            pltpu.VMEM((n_codes, tokens), BF16),
            pltpu.VMEM((n_codes, 256), F32),
            pltpu.VMEM((n_codes, 256), F32),
            pltpu.VMEM((16, 1, 256), F32),
            pltpu.VMEM((16, 1, 256), F32),
            pltpu.VMEM((16, 1, 256), F32),
            pltpu.VMEM((4, 16, 1, 256), F32),
            pltpu.VMEM((4, 16, 1, 256), F32),
            pltpu.VMEM((tokens, width), BF16),
            pltpu.VMEM((2 * subs, CB, width), F32),
            pltpu.VMEM((2 * subs, 8, CB), F32),
            pltpu.VMEM((subs, CB, width), BF16),
            pltpu.VMEM((subs, 8, CB), F32),
            pltpu.VMEM((subs, CB, width), BF16),
            pltpu.VMEM((4 + 2 * subs, 8, CB), F32),
            pltpu.VMEM((subs, CB, width), F32),
            pltpu.SemaphoreType.DMA((48,)),
            pltpu.SemaphoreType.DMA((64,)),
            pltpu.SemaphoreType.DMA((8,)),
            pltpu.SemaphoreType.DMA((8,)),
            pltpu.SemaphoreType.DMA((12,)),
            pltpu.SemaphoreType.DMA((12,)),
        ],
        compiler_params=pltpu.CompilerParams(
            collective_id=0, has_side_effects=True, vmem_limit_bytes=VMEM_LIMIT
        ),
        name="refit",
    )(unit_tokens, codebook, inv_temp.reshape(-1, 128), prior_mass.reshape(-1, 128))
    return out, mass.reshape(-1)


def local(image_tokens, w_in, w_out, w_proj, codebook, inv_temp, prior_mass):
    unit_tokens = encode(image_tokens, w_in, w_out, w_proj)
    return refit(unit_tokens, codebook, inv_temp, prior_mass)


def solution(mesh):
    placed = (P(("dp", "code"), None), P(), P(), P(), P("code", None), P(), P("code"))
    return jax.shard_map(
        local,
        mesh=mesh,
        in_specs=placed,
        out_specs=(P(("code", "dp"), None), P(("code", "dp"))),
        check_vma=False,
    )
```

```python
import functools

import jax
import jax.numpy as jnp
from jax import lax
from jax.experimental import pallas as pl
from jax.experimental.pallas import tpu as pltpu
from jax.sharding import PartitionSpec as P

LOG2E = 1.4426950408889634
F32 = jnp.float32
BF16 = jnp.bfloat16
FT = 512
CH = 1024
CB = 512
MS = 64
VMEM_LIMIT = 67043328


def encode_kernel(x_ref, win_ref, wout_ref, wproj_ref, o_ref, normed, acc):
    step = pl.program_id(0)

    @pl.when(step == 0)
    def _():
        x = x_ref[...].astype(F32)
        mean = jnp.mean(x, axis=1, keepdims=True)
        centered = x - mean
        var = jnp.mean(centered * centered, axis=1, keepdims=True)
        normed[...] = (centered * lax.rsqrt(var + 1e-06)).astype(BF16)
        acc[...] = jnp.zeros_like(acc)

    h = jnp.dot(normed[...], win_ref[...], preferred_element_type=F32)
    h = (0.5 * h * (1.0 + lax.erf(h * 0.7071067811865476))).astype(BF16)
    acc[...] += jnp.dot(h, wout_ref[...], preferred_element_type=F32)

    @pl.when(step == pl.num_programs(0) - 1)
    def _():
        encoded = (x_ref[...].astype(F32) + acc[...]).astype(BF16)
        projected = jnp.dot(encoded, wproj_ref[...], preferred_element_type=F32)
        width = projected.shape[1]
        factor = jnp.sqrt(width / (jnp.sum(projected * projected, axis=1, keepdims=True) + 1e-06))
        o_ref[...] = (projected * factor).astype(BF16)


def encode(x, w_in, w_out, w_proj):
    rows, d = x.shape
    ff, e = w_in.shape[1], w_proj.shape[1]
    return pl.pallas_call(
        encode_kernel,
        grid=(ff // FT,),
        in_specs=[
            pl.BlockSpec((rows, d), lambda i: (0, 0)),
            pl.BlockSpec((d, FT), lambda i: (0, i)),
            pl.BlockSpec((FT, d), lambda i: (i, 0)),
            pl.BlockSpec((d, e), lambda i: (0, 0)),
        ],
        out_specs=pl.BlockSpec((rows, e), lambda i: (0, 0)),
        out_shape=jax.ShapeDtypeStruct((rows, e), BF16),
        scratch_shapes=[pltpu.VMEM((rows, d), BF16), pltpu.VMEM((rows, d), F32)],
        name="encode",
    )(x, w_in, w_out, w_proj)


ORDER_A = [(0, 0), (1, 0), (3, 0), (0, 1), (1, 1), (3, 1), (2, 0), (2, 1)]
ORDER_B = [(0, 0), (0, 1), (1, 0), (1, 1), (3, 0), (3, 1), (2, 0), (2, 1)]


def pick(i, values):
    out = i * 0 + values[0]
    for k, v in enumerate(values[1:], 1):
        out = out + (i == k).astype(jnp.int32) * (v - values[0])
    return out


def refit_kernel(
    ut_ref, book_ref, inv_ref, prior_ref,
    out_ref, mass_ref,
    u_all, codes, p, ls0, ls1, lse, mloc, lx, ly, lz, u2,
    rc, rcm, rx, rxm, sx, sm, totals, wide, macc, mrow, sacc, stage,
    ag_send, ag_recv, st_send, st_recv, rs_send, rs_recv,
):
    n_codes, width = book_ref.shape
    n_blocks = 16
    tb_size = 256
    dp = lax.axis_index("dp")
    code = lax.axis_index("code")
    h = lax.rem(code, 2)
    y = lax.rem(code // 2, 4)
    z = code // 8
    core = lax.rem(dp, 2)
    xlo = dp // 2

    zs = [lax.rem(z + d, 4) for d in range(4)]
    ys = [lax.rem(y + d, 4) for d in range(4)]

    def at(dz, dy, flip=0):
        hh = 1 - h if flip else h
        return (dp, (zs[dz] * 4 + ys[dy]) * 2 + hh)

    partner = (xlo * 2 + (1 - core), code)
    across = ((1 - xlo) * 2 + core, code)

    barrier = pltpu.get_barrier_semaphore()
    peers = [at(0, 0, 1), partner, across]
    peers += [at(d, 0) for d in (1, 2, 3)] + [at(0, d) for d in (1, 2, 3)]
    for peer in peers:
        pl.semaphore_signal(barrier, inc=1, device_id=peer, device_id_type=pl.DeviceIdType.MESH)
    pl.semaphore_wait(barrier, len(peers))

    sent = []

    def place(color, dz, dy):
        return color * 16 + zs[dz % 4] * 4 + ys[dy % 4]

    def view(index, half):
        if half is None:
            return u_all.at[index]
        return u_all.at[index, pl.ds(64 * half, 64)]

    def copy(src, dst, color, dz, dy, half, to):
        slot = ((color * 4 + dz % 4) * 4 + dy % 4) * 2 + (half or 0)
        c = pltpu.make_async_remote_copy(
            src_ref=src, dst_ref=dst, send_sem=ag_send.at[len(sent)], recv_sem=ag_recv.at[slot],
            device_id=to, device_id_type=pl.DeviceIdType.MESH,
        )
        sent.append(half)
        c.start()

    def send(color, dz, dy, half, ez, ey):
        ref = view(place(color, dz, dy), half)
        copy(ref, ref, color, dz - ez, dy - ey, half, at(ez % 4, ey % 4))

    def arrived(color, dz, dy, half=None):
        slot = ((color * 4 + dz) * 4 + dy) * 2 + (half or 0)
        ref = view(place(color, dz, dy), half)
        pltpu.make_async_remote_copy(
            src_ref=ref, dst_ref=ref, send_sem=ag_send.at[0], recv_sem=ag_recv.at[slot],
            device_id=at(1, 0), device_id_type=pl.DeviceIdType.MESH,
        ).wait_recv()

    def both(color, dz, dy, axis):
        for sign in (1, -1):
            send(color, dz, dy, None, *((sign, 0) if axis == "z" else (0, sign)))

    def onward(color, dz, dy, axis):
        arrived(color, dz, dy)
        step = dz if axis == "z" else dy
        half, sign = (0, -1) if step == 1 else (1, 1)
        send(color, dz, dy, half, *((sign, 0) if axis == "z" else (0, sign)))

    def halves(color, dz, dy):
        arrived(color, dz, dy, 0)
        arrived(color, dz, dy, 1)

    def c_start():
        ref = view(place(0, 0, 0), None)
        own = pltpu.make_async_copy(ut_ref, ref, rs_send.at[0])
        own.start()
        own.wait()
        copy(ref, view(place(1, 0, 0), None), 1, 0, 0, None, at(0, 0, 1))
        both(0, 0, 0, "y")
        both(0, 0, 0, "z")

    def c_first():
        for d in (1, 3):
            onward(0, 0, d, "y")
        for d in (1, 3):
            onward(0, d, 0, "z")
            both(0, d, 0, "y")

    def c0():
        arrived(1, 0, 0)
        both(1, 0, 0, "y")
        both(1, 0, 0, "z")
        for d in (1, 3):
            onward(0, 1, d, "y")

    def c1():
        for d in (1, 3):
            onward(0, 3, d, "y")
        halves(0, 2, 0)
        both(0, 2, 0, "y")

    def c2():
        halves(0, 0, 2)
        for d in (1, 3):
            onward(1, 0, d, "y")
            both(1, 0, d, "z")
        for d in (1, 3):
            onward(1, d, 0, "z")

    def c3():
        halves(0, 1, 2)

    def c4():
        halves(0, 3, 2)
        for d in (1, 3):
            onward(0, 2, d, "y")
        halves(1, 0, 2)
        both(1, 0, 2, "z")

    def c5():
        for e in (1, 3):
            for d in (1, 3):
                onward(1, e, d, "z")

    def c6():
        halves(0, 2, 2)

    def c7():
        for e in (1, 3):
            onward(1, e, 2, "z")

    def c13():
        halves(1, 2, 0)
        halves(1, 2, 1)
        halves(1, 2, 3)

    def c14():
        halves(1, 2, 2)

    comm = {0: c0, 1: c1, 2: c2, 3: c3, 4: c4, 5: c5, 6: c6, 7: c7, 13: c13, 14: c14}

    c_start()

    def unit_body(i, _):
        r = pl.ds(pl.multiple_of(i * 256, 256), 256)
        b = book_ref[r, :].astype(F32)
        codes[r, :] = (b * lax.rsqrt(jnp.mean(b * b, axis=1, keepdims=True) + 1e-06)).astype(BF16)
        return 0

    lax.fori_loop(0, n_codes // 256, unit_body, 0)
    c_first()

    rel_z = [a for a, _ in ORDER_A + ORDER_B]
    rel_p = [b for _, b in ORDER_A + ORDER_B]

    def block_at(i):
        color = i // 8
        zz = lax.rem(z + pick(i, rel_z), 4)
        pair = lax.rem(y // 2 + pick(i, rel_p), 2)
        hh = jnp.where(color == 0, h, 1 - h)
        return color * 8 + zz * 2 + pair, dp * 32 + (zz * 4 + pair * 2) * 2 + hh

    neg = jnp.full((8, tb_size), -jnp.inf, F32)

    def logits_of(tb, q, dest, peak):
        tokens = u_all[pl.ds(2 * tb, 2)].reshape(tb_size, width)
        l = lax.dot_general(
            codes[q * CH:(q + 1) * CH, :], tokens, (((1,), (1,)), ((), ())), preferred_element_type=F32
        )
        dest[q * CH:(q + 1) * CH, :] = l
        return jnp.maximum(peak, jnp.max(l.reshape(CH // 8, 8, tb_size), axis=0))

    def step(i, peak8, cur, nxt):
        tb, row = block_at(i)
        nxt_tb, _ = block_at(jnp.minimum(i + 1, n_blocks - 1))
        scale = jnp.concatenate([inv_ref[pl.ds(row, 1), :], inv_ref[pl.ds(row + 2, 1), :]], axis=1)
        scale = scale * (LOG2E / width)
        peak = jnp.max(peak8, axis=0, keepdims=True) * scale
        columns = pl.ds(pl.multiple_of(tb * tb_size, tb_size), tb_size)
        new_peak = neg
        total = jnp.zeros((8, tb_size), F32)
        for q in range(n_codes // CH):
            new_peak = logits_of(nxt_tb, q, nxt, new_peak)
            e = jnp.exp2(cur[q * CH:(q + 1) * CH, :] * scale - peak)
            p[q * CH:(q + 1) * CH, columns] = e.astype(BF16)
            total = total + jnp.sum(e.reshape(CH // 8, 8, tb_size), axis=0)
        mloc[tb] = peak
        lse[tb] = peak + jnp.log2(jnp.sum(total, axis=0, keepdims=True))
        return new_peak

    first, _ = block_at(h * 0)
    peak = neg
    for q in range(n_codes // CH):
        peak = logits_of(first, q, ls0, peak)

    def two_steps(j, peak8):
        for s, (cur, nxt) in enumerate(((ls0, ls1), (ls1, ls0))):
            for k, fn in comm.items():
                if k % 2 == s:
                    pl.when(j == k // 2)(fn)
            peak8 = step(2 * j + s, peak8, cur, nxt)
        return peak8

    lax.fori_loop(0, n_blocks // 2, two_steps, peak)

    stat_sent = []

    def stat_send(src, dst, slot, to):
        c = pltpu.make_async_remote_copy(
            src_ref=src, dst_ref=dst, send_sem=st_send.at[slot], recv_sem=st_recv.at[slot],
            device_id=to, device_id_type=pl.DeviceIdType.MESH,
        )
        stat_sent.append(c)
        c.start()
        return c

    cx = [
        stat_send(lse.at[pl.ds(0, 8)], lx.at[pl.ds(8, 8)], 0, at(0, 0, 1)),
        stat_send(lse.at[pl.ds(8, 8)], lx.at[pl.ds(0, 8)], 1, at(0, 0, 1)),
    ]
    for c in cx:
        c.wait()
    parts = [lse[...], lx[...]]
    top = jnp.maximum(*parts)
    ly[0] = top + jnp.log2(sum(jnp.exp2(v - top) for v in parts))
    cy = [stat_send(ly.at[0], ly.at[d], 1 + d, at(0, d)) for d in (1, 2, 3)]
    for c in cy:
        c.wait()
    parts = [ly[d] for d in range(4)]
    top = functools.reduce(jnp.maximum, parts)
    lz[0] = top + jnp.log2(sum(jnp.exp2(v - top) for v in parts))
    cz = [stat_send(lz.at[0], lz.at[d], 4 + d, at(d, 0)) for d in (1, 2, 3)]
    for c in cz:
        c.wait()
    parts = [lz[d] for d in range(4)]
    top = functools.reduce(jnp.maximum, parts)
    mloc[...] = jnp.exp2(mloc[...] - (top + jnp.log2(sum(jnp.exp2(v - top) for v in parts))))

    for k, half in enumerate(sent):
        ref = view(place(0, 0, 0), half)
        pltpu.make_async_remote_copy(
            src_ref=ref, dst_ref=ref, send_sem=ag_send.at[k], recv_sem=ag_recv.at[0],
            device_id=at(1, 0), device_id_type=pl.DeviceIdType.MESH,
        ).wait_send()

    def scale_body(tb, _):
        w = jnp.broadcast_to(mloc[tb], (128, tb_size)).T
        w = jnp.concatenate([w, w], axis=1)
        rows = pl.ds(pl.multiple_of(tb * tb_size, tb_size), tb_size)
        tokens = u_all[pl.ds(2 * tb, 2)].reshape(tb_size, width)
        u2[rows, :] = (tokens.astype(F32) * w).astype(BF16)
        for k in range(2):
            wide[2 * tb + k] = jnp.broadcast_to(mloc[tb][:, k * 128:(k + 1) * 128], (16, 128)).astype(BF16)
        return 0

    lax.fori_loop(0, n_blocks, scale_body, 0)

    per = n_codes // 4
    subs = per // CB

    def sums_of(first_row):
        r = pl.ds(pl.multiple_of(first_row, CB), CB)
        s = jnp.dot(p[r, :], u2[...], preferred_element_type=F32)
        for q in range(CB // MS):
            rq = pl.ds(pl.multiple_of(first_row + q * MS, MS), MS)
            acc = None
            for j in range(0, n_blocks * 2, 2):
                pair = [
                    p[rq, k * 128:(k + 1) * 128].reshape(MS // 16, 16, 128) * wide[k][None] for k in (j, j + 1)
                ]
                v = (pair[0] + pair[1]).astype(F32)
                acc = v if acc is None else acc + v
            macc[q * MS:(q + 1) * MS, :] = acc.reshape(MS, 128)
        col = jnp.broadcast_to(jnp.sum(macc[...], axis=1, keepdims=True), (CB, 128))
        for k in range(CB // 128):
            mrow[:, k * 128:(k + 1) * 128] = col[k * 128:(k + 1) * 128, :].T[0:8, :]
        sacc[...] = s

    def reduce_copy(src, dst, slot, to):
        return pltpu.make_async_remote_copy(
            src_ref=src, dst_ref=dst, send_sem=rs_send.at[slot], recv_sem=rs_recv.at[slot],
            device_id=to, device_id_type=pl.DeviceIdType.MESH,
        )

    def to_partner(slot):
        return [
            reduce_copy(stage.at[slot], rc.at[slot], slot, partner),
            reduce_copy(sm.at[slot], rcm.at[slot], 4 + slot, partner),
        ]

    def to_across(b):
        return [
            reduce_copy(sx.at[b], rx.at[b], 8 + b, across),
            reduce_copy(sm.at[4 + b], rxm.at[b], 10 + b, across),
        ]

    def chunk(c, _):
        side = c // (2 * subs)
        ours = lax.rem(c // subs, 2)
        b = lax.rem(c, subs)
        slot = side * subs + b
        chip = xlo + (1 - side) * (1 - 2 * xlo)
        owner = chip * 2 + core + (1 - ours) * (1 - 2 * core)
        sums_of(owner * per + b * CB)

        @pl.when(ours == 0)
        def _():
            stage[slot] = sacc[...].astype(BF16)
            sm[slot] = mrow[...]
            for cp in to_partner(slot):
                cp.start()

        @pl.when(ours == 1)
        def _():
            for cp in to_partner(slot):
                cp.wait_recv()

        @pl.when((ours == 1) & (side == 0))
        def _():
            sx[b] = (sacc[...] + rc[slot].astype(F32)).astype(BF16)
            sm[4 + b] = mrow[...] + rcm[slot]
            for cp in to_across(b):
                cp.start()

        @pl.when((ours == 1) & (side == 1))
        def _():
            totals[b] = sacc[...] + rc[slot].astype(F32)
            sm[4 + subs + b] = mrow[...] + rcm[slot]

        return 0

    lax.fori_loop(0, 4 * subs, chunk, 0)

    def column(row):
        c = jnp.broadcast_to(row, (128, 128)).T
        return jnp.concatenate([c, c], axis=1)

    for b in range(subs):
        for cp in to_across(b):
            cp.wait_recv()
        m = sm[4 + subs + b] + rxm[b]
        for k in range(CB // 128):
            local = b * CB + k * 128
            part = slice(k * 128, (k + 1) * 128)
            index = b * (CB // 128) + k
            m_row = m[0:1, part]
            mass_ref[index:index + 1, :] = m_row
            prior = column(prior_ref[pl.ds(dp * (per // 128) + index, 1), :])
            book = book_ref[pl.ds(pl.multiple_of(dp * per + local, 128), 128), :].astype(F32)
            s = totals[b, part, :] + rx[b, part, :].astype(F32)
            out_ref[local:local + 128, :] = (prior * book + s) / (prior + column(m_row))

    for slot in range(2 * subs):
        for cp in to_partner(slot):
            cp.wait_send()
    for b in range(subs):
        for cp in to_across(b):
            cp.wait_send()


def hand_on_kernel(a_ref, b_ref, a_out, b_out):
    a_out[...] = a_ref[...]
    b_out[...] = b_ref[...]


def hand_on(a, b):
    steps = 4
    rows = a.shape[0] // steps
    specs = [
        pl.BlockSpec((rows, a.shape[1]), lambda i: (i, 0)),
        pl.BlockSpec(b.shape, lambda i: (0, 0)),
    ]
    return pl.pallas_call(
        hand_on_kernel, grid=(steps,), in_specs=specs, out_specs=specs,
        out_shape=[jax.ShapeDtypeStruct(v.shape, v.dtype) for v in (a, b)], name="hand_on",
    )(a, b)


def refit(unit_tokens, codebook, inv_temp, prior_mass):
    n_codes, width = codebook.shape
    tokens = unit_tokens.shape[0] * 32
    per = n_codes // 4
    subs = per // CB
    vmem = pl.BlockSpec(memory_space=pltpu.VMEM)
    out, mass = pl.pallas_call(
        refit_kernel,
        in_specs=[vmem] * 4,
        out_specs=[vmem] * 2,
        out_shape=[
            jax.ShapeDtypeStruct((per, width), F32),
            jax.ShapeDtypeStruct((per // 128, 128), F32),
        ],
        scratch_shapes=[
            pltpu.VMEM((32, 128, width), BF16),
            pltpu.VMEM((n_codes, width), BF16),
            pltpu.VMEM((n_codes, tokens), BF16),
            pltpu.VMEM((n_codes, 256), F32),
            pltpu.VMEM((n_codes, 256), F32),
            pltpu.VMEM((16, 1, 256), F32),
            pltpu.VMEM((16, 1, 256), F32),
            pltpu.VMEM((16, 1, 256), F32),
            pltpu.VMEM((4, 16, 1, 256), F32),
            pltpu.VMEM((4, 16, 1, 256), F32),
            pltpu.VMEM((tokens, width), BF16),
            pltpu.VMEM((2 * subs, CB, width), BF16),
            pltpu.VMEM((2 * subs, 8, CB), F32),
            pltpu.VMEM((subs, CB, width), BF16),
            pltpu.VMEM((subs, 8, CB), F32),
            pltpu.VMEM((subs, CB, width), BF16),
            pltpu.VMEM((4 + 2 * subs, 8, CB), F32),
            pltpu.VMEM((subs, CB, width), F32),
            pltpu.VMEM((32, 16, 128), BF16),
            pltpu.VMEM((CB, 128), F32),
            pltpu.VMEM((8, CB), F32),
            pltpu.VMEM((CB, width), F32),
            pltpu.VMEM((2 * subs, CB, width), BF16),
            pltpu.SemaphoreType.DMA((48,)),
            pltpu.SemaphoreType.DMA((64,)),
            pltpu.SemaphoreType.DMA((8,)),
            pltpu.SemaphoreType.DMA((8,)),
            pltpu.SemaphoreType.DMA((12,)),
            pltpu.SemaphoreType.DMA((12,)),
        ],
        compiler_params=pltpu.CompilerParams(
            collective_id=0, has_side_effects=True, vmem_limit_bytes=VMEM_LIMIT
        ),
        name="refit",
    )(unit_tokens, codebook, inv_temp.reshape(-1, 128), prior_mass.reshape(-1, 128))
    out, mass = hand_on(out, mass)
    return out, mass.reshape(-1)


def local(image_tokens, w_in, w_out, w_proj, codebook, inv_temp, prior_mass):
    unit_tokens = encode(image_tokens, w_in, w_out, w_proj)
    return refit(unit_tokens, codebook, inv_temp, prior_mass)


def solution(mesh):
    placed = (P(("dp", "code"), None), P(), P(), P(), P("code", None), P(), P("code"))
    return jax.shard_map(
        local,
        mesh=mesh,
        in_specs=placed,
        out_specs=(P(("code", "dp"), None), P(("code", "dp"))),
        check_vma=False,
    )
```
